768 devices in a mesh: segment: 32 (over z_lo, y), mp: 24 (over z_hi, x, core).
Axes of the slice: x: 4, y: 8, z: 12 (z_hi: 3, z_lo: 4; z = z_hi * 4 + z_lo), core: 2. Of those that a mesh axis runs over, the one named last changes fastest.
Arguments:
- enc_out: bfloat16 [2, 192, 4096], P(None, 'mp', 'segment'), may hold values from -6 to 6
- dec_in: bfloat16 [2, 32, 512, 4096], P(None, 'segment'), may hold values from -43 to 43
- grad_context: bfloat16 [2, 32, 512, 3072], P(None, 'segment', None, 'mp'), may hold values from -6 to 6
- w_query: bfloat16 [32, 4096, 3072], P('segment', None, 'mp'), may hold values from -0.09375 to 0.09375
- w_keyval: bfloat16 [32, 4096, 2, 3072], P('segment', None, None, 'mp'), may hold values from -0.09375 to 0.09375
- src_len: int32 [2], replicated, may hold values from 48 to 192, as said below
Outputs:
- context: bfloat16 [2, 32, 512, 3072], P(None, 'segment', None, 'mp')
- d_enc: float32 [2, 192, 4096], P(None, 'mp', 'segment')
The draws below stay inside these ranges and needn't reach their ends.
Inputs may be any that keep to these rules, and one draw needn't show every extreme that they name: `src_len`: one micro-batch is unpadded.
All inputs are finite; a program needn't handle non-finite values.
Results may differ from the reference program's by a relative error of at most 0.017.
The reference program's roundings to bfloat16 on the way (of `query`, `keyval`, `attend_low`, `dscore` and `dkeyval`) count: a program that leaves them out, or rounds other values in their place, can miss the bound.
Values may be sent and summed in bfloat16 or wider, within the bound.
A program may use at most 64 MiB of HBM per device.

```python
import math
import jax
import jax.numpy as jnp
from jax import lax

D = 4096
HD = 64
MB = 2
TGT = 512
SRC = 192
HEADS = 48
LAYERS = 32


def draw_dec_in(key, part):
    shape = (MB, LAYERS, TGT, D)
    first_key = jax.random.fold_in(key, 11)
    values = jax.random.truncated_normal(first_key, -6.0, 6.0, shape, jnp.float32)
    return values.astype(jnp.bfloat16)


def draw_src_len(key, part):
    lengths = jax.random.randint(jax.random.fold_in(key, 21), (MB,), SRC // 4, SRC + 1)
    full_one = jax.random.randint(jax.random.fold_in(key, 22), (), 0, MB)
    return jnp.where(jnp.arange(MB) == full_one, SRC, lengths).astype(jnp.int32)


def block_scale(stream_key, dims, cuts, smallest, largest):
    factor_of, own = 1.0, jax.random.fold_in(stream_key, 6)
    for dim, shards_of in cuts:
        draws = jnp.exp(jax.random.uniform(jax.random.fold_in(own, dim), (shards_of,), jnp.float32, smallest / len(cuts), largest / len(cuts)))
        factor_of = factor_of * jnp.repeat(draws, dims[dim] // shards_of).reshape([-1 if axis == dim else 1 for axis in range(len(dims))])
    return factor_of


def scatter_about(stream_key, shape, deviation, limit, split=(), dtype=jnp.bfloat16):
    loudness = block_scale(stream_key, shape, split, -0.22, 0.18) if split else 1.0
    values = jax.random.normal(stream_key, shape, jnp.float32) * deviation * loudness
    return jnp.minimum(jnp.maximum(values, -limit), limit).astype(dtype)


def setup_inputs(seed: int = 0) -> dict:
    seeds = jax.random.split(jax.random.key(seed), 7)
    return {
        "enc_out": scatter_about(seeds[0], (MB, SRC, D), 1.0, 6.0, ((1, 24), (2, 32))),
        "dec_in": draw_dec_in(jax.random.fold_in(seeds[6], 71), 0),
        "grad_context": scatter_about(seeds[2], (MB, LAYERS, TGT, HEADS * HD), 1.0, 6.0, ((1, 32), (3, 24))),
        "w_query": scatter_about(seeds[3], (LAYERS, D, HEADS * HD), D ** -0.5, 0.09375, ((0, 32), (2, 24))),
        "w_keyval": scatter_about(seeds[4], (LAYERS, D, 2, HEADS * HD), D ** -0.5, 0.09375, ((0, 32), (3, 24))),
        "src_len": draw_src_len(jax.random.fold_in(seeds[6], 71), 0),
    }


def attend_pass(query, keyval, cotangent, usable):
    num_batch, num_tgt, width = query.shape
    num_heads = width // HD
    inv_root = 1.0 / math.sqrt(HD)
    query_heads = query.reshape(num_batch, num_tgt, num_heads, HD).astype(jnp.float32)
    key_heads = keyval[:, :, 0].reshape(num_batch, -1, num_heads, HD).astype(jnp.float32)
    value_heads = keyval[:, :, 1].reshape(num_batch, -1, num_heads, HD).astype(jnp.float32)
    cot_heads = cotangent.reshape(num_batch, num_tgt, num_heads, HD).astype(jnp.float32)
    scores = jnp.einsum('bthe,bshe->bhts', query_heads, key_heads) * inv_root
    scores = jnp.where(usable[:, None, None, :], scores, jnp.float32(-1e+30))
    shifted = scores - lax.optimization_barrier(jnp.max(scores, axis=-1, keepdims=True))
    raised = jnp.exp(shifted)
    attend = raised / lax.optimization_barrier(jnp.sum(raised, axis=-1, keepdims=True))
    attend_low = attend.astype(jnp.bfloat16)
    context = jnp.einsum('bhts,bshe->bthe', attend_low.astype(jnp.float32), value_heads).astype(jnp.bfloat16)
    slope = jnp.einsum('bthe,bshe->bhts', cot_heads, value_heads)
    row_dot = jnp.einsum('bthe,bthe->bht', cot_heads, context.astype(jnp.float32))
    dscore = (attend * (slope - row_dot[..., None]) * inv_root).astype(jnp.bfloat16)
    dkey = jnp.einsum('bhts,bthe->bshe', dscore.astype(jnp.float32), query_heads).astype(jnp.bfloat16)
    dvalue = jnp.einsum('bhts,bthe->bshe', attend_low.astype(jnp.float32), cot_heads).astype(jnp.bfloat16)
    dkeyval = jnp.stack([dkey.reshape(num_batch, -1, width), dvalue.reshape(num_batch, -1, width)], axis=2)
    return (context.reshape(num_batch, num_tgt, width), dkeyval)

def reference(enc_out, dec_in, grad_context, w_query, w_keyval, src_len):
    usable = jnp.arange(SRC)[None, :] < src_len[:, None]
    encoder = enc_out.astype(jnp.float32)

    def one_layer(carried, layer_in):
        inputs, cotangent, query_w, keyval_w = layer_in
        query = jnp.einsum('btd,dh->bth', inputs.astype(jnp.float32), query_w.astype(jnp.float32)).astype(jnp.bfloat16)
        keyval = jnp.einsum('bsd,dch->bsch', encoder, keyval_w.astype(jnp.float32)).astype(jnp.bfloat16)
        context, dkeyval = attend_pass(query, keyval, cotangent, usable)
        layer_grad = jnp.einsum('bsch,dch->bsd', dkeyval.astype(jnp.float32), keyval_w.astype(jnp.float32))
        return (carried + layer_grad, context)
    zero_grad = jnp.zeros((MB, SRC, D), jnp.float32)
    d_enc, contexts = lax.scan(one_layer, zero_grad, (jnp.swapaxes(dec_in, 0, 1), jnp.swapaxes(grad_context, 0, 1), w_query, w_keyval))
    return (jnp.swapaxes(contexts, 0, 1), d_enc)
```

```python
import math

import jax
import jax.numpy as jnp
from jax import lax
from jax.sharding import PartitionSpec as P

HD = 64


def attend_pass(query, keyval, cotangent, usable):
    num_batch, num_tgt, width = query.shape
    num_heads = width // HD
    inv_root = 1.0 / math.sqrt(HD)
    query_heads = query.reshape(num_batch, num_tgt, num_heads, HD)
    key_heads = keyval[:, :, 0].reshape(num_batch, -1, num_heads, HD)
    value_heads = keyval[:, :, 1].reshape(num_batch, -1, num_heads, HD)
    cot_heads = cotangent.reshape(num_batch, num_tgt, num_heads, HD)
    scores = (
        jnp.einsum("bthe,bshe->bhts", query_heads, key_heads, preferred_element_type=jnp.float32)
        * inv_root
    )
    scores = jnp.where(usable[:, None, None, :], scores, jnp.float32(-1e30))
    shifted = scores - jnp.max(scores, axis=-1, keepdims=True)
    raised = jnp.exp(shifted)
    attend = raised / jnp.sum(raised, axis=-1, keepdims=True)
    attend_low = attend.astype(jnp.bfloat16)
    context = jnp.einsum(
        "bhts,bshe->bthe", attend_low, value_heads, preferred_element_type=jnp.float32
    ).astype(jnp.bfloat16)
    slope = jnp.einsum(
        "bthe,bshe->bhts", cot_heads, value_heads, preferred_element_type=jnp.float32
    )
    row_dot = jnp.einsum("bthe,bthe->bht", cot_heads, context, preferred_element_type=jnp.float32)
    dscore = (attend * (slope - row_dot[..., None]) * inv_root).astype(jnp.bfloat16)
    dkey = jnp.einsum(
        "bhts,bthe->bshe", dscore, query_heads, preferred_element_type=jnp.float32
    ).astype(jnp.bfloat16)
    dvalue = jnp.einsum(
        "bhts,bthe->bshe", attend_low, cot_heads, preferred_element_type=jnp.float32
    ).astype(jnp.bfloat16)
    dkeyval = jnp.stack(
        [dkey.reshape(num_batch, -1, width), dvalue.reshape(num_batch, -1, width)], axis=2
    )
    return (context.reshape(num_batch, num_tgt, width), dkeyval)


def local(enc_out, dec_in, grad_context, w_query, w_keyval, src_len):
    inputs = dec_in[:, 0]
    cotangent = grad_context[:, 0]
    query_w = w_query[0]
    keyval_w = w_keyval[0]
    query = jnp.einsum("btd,dh->bth", inputs, query_w, preferred_element_type=jnp.float32).astype(
        jnp.bfloat16
    )
    nb, ns, nd = enc_out.shape
    n_mp = lax.axis_size("mp")
    n_seg = lax.axis_size("segment")
    gathered = lax.all_gather(enc_out, ("mp", "segment"), axis=0, tiled=False)
    encoder = (
        gathered.reshape(n_mp, n_seg, nb, ns, nd)
        .transpose(2, 0, 3, 1, 4)
        .reshape(nb, n_mp * ns, n_seg * nd)
    )
    keyval = jnp.einsum(
        "bsd,dch->bsch",
        encoder,
        keyval_w,
        preferred_element_type=jnp.float32,
    ).astype(jnp.bfloat16)
    total_src = keyval.shape[1]
    usable = jnp.arange(total_src)[None, :] < src_len[:, None]
    context, dkeyval = attend_pass(query, keyval, cotangent, usable)
    layer_grad = jnp.einsum("bsch,dch->bsd", dkeyval, keyval_w, preferred_element_type=jnp.float32)
    blocks = (
        layer_grad.reshape(nb, n_mp, ns, n_seg, nd)
        .transpose(1, 3, 0, 2, 4)
        .reshape(n_mp * n_seg, nb, ns, nd)
    )
    d_enc = lax.psum_scatter(blocks, ("mp", "segment"), scatter_dimension=0, tiled=False)
    return (context[:, None], d_enc)


def solution(mesh):
    placed = (
        P(None, "mp", "segment"),
        P(None, "segment", None, None),
        P(None, "segment", None, "mp"),
        P("segment", None, "mp"),
        P("segment", None, None, "mp"),
        P(),
    )
    return jax.shard_map(
        local,
        mesh=mesh,
        in_specs=placed,
        out_specs=(P(None, "segment", None, "mp"), P(None, "mp", "segment")),
        check_vma=False,
    )
```

```python
import math

import jax
import jax.numpy as jnp
from jax import lax
from jax.sharding import PartitionSpec as P
from jax.experimental import pallas as pl
from jax.experimental.pallas import tpu as pltpu
import functools

HD = 64


def attend_pass(query, keyval, cotangent, usable):
    num_batch, num_tgt, width = query.shape
    num_heads = width // HD
    inv_root = 1.0 / math.sqrt(HD)
    query_heads = query.reshape(num_batch, num_tgt, num_heads, HD)
    key_heads = keyval[:, :, 0].reshape(num_batch, -1, num_heads, HD)
    value_heads = keyval[:, :, 1].reshape(num_batch, -1, num_heads, HD)
    cot_heads = cotangent.reshape(num_batch, num_tgt, num_heads, HD)
    scores = (
        jnp.einsum("bthe,bshe->bhts", query_heads, key_heads, preferred_element_type=jnp.float32)
        * inv_root
    )
    scores = jnp.where(usable[:, None, None, :], scores, jnp.float32(-1e30))
    shifted = scores - jnp.max(scores, axis=-1, keepdims=True)
    raised = jnp.exp(shifted)
    attend = raised / jnp.sum(raised, axis=-1, keepdims=True)
    attend_low = attend.astype(jnp.bfloat16)
    context = jnp.einsum(
        "bhts,bshe->bthe", attend_low, value_heads, preferred_element_type=jnp.float32
    ).astype(jnp.bfloat16)
    slope = jnp.einsum(
        "bthe,bshe->bhts", cot_heads, value_heads, preferred_element_type=jnp.float32
    )
    row_dot = jnp.einsum("bthe,bthe->bht", cot_heads, context, preferred_element_type=jnp.float32)
    dscore = (attend * (slope - row_dot[..., None]) * inv_root).astype(jnp.bfloat16)
    dkey = jnp.einsum(
        "bhts,bthe->bshe", dscore, query_heads, preferred_element_type=jnp.float32
    ).astype(jnp.bfloat16)
    dvalue = jnp.einsum(
        "bhts,bthe->bshe", attend_low, cot_heads, preferred_element_type=jnp.float32
    ).astype(jnp.bfloat16)
    dkeyval = jnp.stack(
        [dkey.reshape(num_batch, -1, width), dvalue.reshape(num_batch, -1, width)], axis=2
    )
    return (context.reshape(num_batch, num_tgt, width), dkeyval)


def _exchange_kernel(axis, n, gather, x_ref, y_ref, send_sem, recv_sem, local_sem):
    me = lax.axis_index(axis)
    mesh_ids = pl.DeviceIdType.MESH
    barrier = pltpu.get_barrier_semaphore()

    def greet(k, carry):
        peer = lax.rem(me + k, n)
        pl.semaphore_signal(barrier, inc=1, device_id={axis: peer}, device_id_type=mesh_ids)
        return carry

    lax.fori_loop(1, n, greet, 0)
    pl.semaphore_wait(barrier, n - 1)

    def send(k, carry):
        peer = lax.rem(me + k, n)
        block = x_ref if gather else x_ref.at[peer]
        pltpu.make_async_remote_copy(
            src_ref=block,
            dst_ref=y_ref.at[me],
            send_sem=send_sem,
            recv_sem=recv_sem,
            device_id={axis: peer},
            device_id_type=mesh_ids,
        ).start()
        return carry

    lax.fori_loop(1, n, send, 0)
    own = pltpu.make_async_copy(x_ref if gather else x_ref.at[me], y_ref.at[me], local_sem)
    own.start()
    own.wait()
    every = pltpu.make_async_remote_copy(
        src_ref=y_ref.at[pl.ds(0, n - 1)],
        dst_ref=y_ref.at[pl.ds(0, n - 1)],
        send_sem=send_sem,
        recv_sem=recv_sem,
        device_id={axis: lax.rem(me + 1, n)},
        device_id_type=mesh_ids,
    )
    every.wait_send()
    every.wait_recv()


def exchange(x, axis, n, cid, gather):
    block = x.shape if gather else x.shape[1:]
    out_shape = jax.ShapeDtypeStruct((n,) + tuple(block), x.dtype)
    return pl.pallas_call(
        functools.partial(_exchange_kernel, axis, n, gather),
        out_shape=out_shape,
        in_specs=[pl.BlockSpec(memory_space=pl.ANY)],
        out_specs=pl.BlockSpec(memory_space=pl.ANY),
        scratch_shapes=[
            pltpu.SemaphoreType.DMA,
            pltpu.SemaphoreType.DMA,
            pltpu.SemaphoreType.DMA,
        ],
        compiler_params=pltpu.CompilerParams(collective_id=cid, has_side_effects=True),
    )(x)


def local(enc_out, dec_in, grad_context, w_query, w_keyval, src_len):
    inputs = dec_in[:, 0]
    cotangent = grad_context[:, 0]
    query_w = w_query[0]
    keyval_w = w_keyval[0]
    query = jnp.einsum("btd,dh->bth", inputs, query_w, preferred_element_type=jnp.float32).astype(
        jnp.bfloat16
    )
    nb, ns, nd = enc_out.shape
    n_mp = lax.axis_size("mp")
    n_seg = lax.axis_size("segment")
    by_feature = exchange(enc_out, "segment", n_seg, 0, True)
    features = by_feature.transpose(1, 2, 0, 3).reshape(nb, ns, n_seg * nd)
    by_source = exchange(features, "mp", n_mp, 1, True)
    encoder = by_source.transpose(1, 0, 2, 3).reshape(nb, n_mp * ns, n_seg * nd)
    keyval = jnp.einsum(
        "bsd,dch->bsch",
        encoder,
        keyval_w,
        preferred_element_type=jnp.float32,
    ).astype(jnp.bfloat16)
    total_src = keyval.shape[1]
    usable = jnp.arange(total_src)[None, :] < src_len[:, None]
    context, dkeyval = attend_pass(query, keyval, cotangent, usable)
    grad_blocks = dkeyval.reshape(nb, n_mp, ns, *dkeyval.shape[2:])
    layer_grad = jnp.einsum(
        "bmsch,dch->mbsd", grad_blocks, keyval_w, preferred_element_type=jnp.float32
    )
    by_heads = exchange(layer_grad, "mp", n_mp, 2, False).sum(axis=0)
    split = by_heads.reshape(nb, ns, n_seg, nd).transpose(2, 0, 1, 3)
    d_enc = exchange(split, "segment", n_seg, 3, False).sum(axis=0)
    return (context[:, None], d_enc)


def solution(mesh):
    placed = (
        P(None, "mp", "segment"),
        P(None, "segment", None, None),
        P(None, "segment", None, "mp"),
        P("segment", None, "mp"),
        P("segment", None, None, "mp"),
        P(),
    )
    return jax.shard_map(
        local,
        mesh=mesh,
        in_specs=placed,
        out_specs=(P(None, "segment", None, "mp"), P(None, "mp", "segment")),
        check_vma=False,
    )
```

```python
import math

import jax
import jax.numpy as jnp
from jax import lax
from jax.sharding import PartitionSpec as P
from jax.experimental import pallas as pl
from jax.experimental.pallas import tpu as pltpu
import functools

HD = 64


def attend_pass(query, keyval, cotangent, usable):
    num_batch, num_tgt, width = query.shape
    num_heads = width // HD
    inv_root = 1.0 / math.sqrt(HD)
    query_heads = query.reshape(num_batch, num_tgt, num_heads, HD)
    key_heads = keyval[:, :, 0].reshape(num_batch, -1, num_heads, HD)
    value_heads = keyval[:, :, 1].reshape(num_batch, -1, num_heads, HD)
    cot_heads = cotangent.reshape(num_batch, num_tgt, num_heads, HD)
    scores = (
        jnp.einsum("bthe,bshe->bhts", query_heads, key_heads, preferred_element_type=jnp.float32)
        * inv_root
    )
    scores = jnp.where(usable[:, None, None, :], scores, jnp.float32(-1e30))
    shifted = scores - jnp.max(scores, axis=-1, keepdims=True)
    raised = jnp.exp(shifted)
    attend = raised / jnp.sum(raised, axis=-1, keepdims=True)
    attend_low = attend.astype(jnp.bfloat16)
    context = jnp.einsum(
        "bhts,bshe->bthe", attend_low, value_heads, preferred_element_type=jnp.float32
    ).astype(jnp.bfloat16)
    slope = jnp.einsum(
        "bthe,bshe->bhts", cot_heads, value_heads, preferred_element_type=jnp.float32
    )
    row_dot = jnp.einsum("bthe,bthe->bht", cot_heads, context, preferred_element_type=jnp.float32)
    dscore = (attend * (slope - row_dot[..., None]) * inv_root).astype(jnp.bfloat16)
    dkey = jnp.einsum(
        "bhts,bthe->bshe", dscore, query_heads, preferred_element_type=jnp.float32
    ).astype(jnp.bfloat16)
    dvalue = jnp.einsum(
        "bhts,bthe->bshe", attend_low, cot_heads, preferred_element_type=jnp.float32
    ).astype(jnp.bfloat16)
    dkeyval = jnp.stack(
        [dkey.reshape(num_batch, -1, width), dvalue.reshape(num_batch, -1, width)], axis=2
    )
    return (context.reshape(num_batch, num_tgt, width), dkeyval)


def _exchange_kernel(axis, stride, count, gather, x_ref, y_ref, send_sem, recv_sem, local_sem):
    me = lax.axis_index(axis)
    digit = lax.rem(lax.div(me, stride), count)
    base = me - digit * stride
    mesh_ids = pl.DeviceIdType.MESH
    barrier = pltpu.get_barrier_semaphore()

    def peer_of(k):
        return base + lax.rem(digit + k, count) * stride

    def greet(k, carry):
        pl.semaphore_signal(barrier, inc=1, device_id={axis: peer_of(k)}, device_id_type=mesh_ids)
        return carry

    lax.fori_loop(1, count, greet, 0)
    pl.semaphore_wait(barrier, count - 1)

    def send(k, carry):
        slot = lax.rem(digit + k, count)
        block = x_ref if gather else x_ref.at[slot]
        pltpu.make_async_remote_copy(
            src_ref=block,
            dst_ref=y_ref.at[digit],
            send_sem=send_sem,
            recv_sem=recv_sem,
            device_id={axis: base + slot * stride},
            device_id_type=mesh_ids,
        ).start()
        return carry

    lax.fori_loop(1, count, send, 0)
    own = pltpu.make_async_copy(x_ref if gather else x_ref.at[digit], y_ref.at[digit], local_sem)
    own.start()
    own.wait()
    every = pltpu.make_async_remote_copy(
        src_ref=y_ref.at[pl.ds(0, count - 1)],
        dst_ref=y_ref.at[pl.ds(0, count - 1)],
        send_sem=send_sem,
        recv_sem=recv_sem,
        device_id={axis: peer_of(1)},
        device_id_type=mesh_ids,
    )
    every.wait_send()
    every.wait_recv()


def exchange(x, axis, stride, count, cid, gather):
    block = x.shape if gather else x.shape[1:]
    out_shape = jax.ShapeDtypeStruct((count,) + tuple(block), x.dtype)
    return pl.pallas_call(
        functools.partial(_exchange_kernel, axis, stride, count, gather),
        out_shape=out_shape,
        in_specs=[pl.BlockSpec(memory_space=pl.ANY)],
        out_specs=pl.BlockSpec(memory_space=pl.ANY),
        scratch_shapes=[
            pltpu.SemaphoreType.DMA,
            pltpu.SemaphoreType.DMA,
            pltpu.SemaphoreType.DMA,
        ],
        compiler_params=pltpu.CompilerParams(collective_id=cid, has_side_effects=True),
    )(x)


def local(enc_out, dec_in, grad_context, w_query, w_keyval, src_len):
    inputs = dec_in[:, 0]
    cotangent = grad_context[:, 0]
    query_w = w_query[0]
    keyval_w = w_keyval[0]
    query = jnp.einsum("btd,dh->bth", inputs, query_w, preferred_element_type=jnp.float32).astype(
        jnp.bfloat16
    )
    nb, ns, nd = enc_out.shape
    n_mp = lax.axis_size("mp")
    n_seg = lax.axis_size("segment")
    n_core = 2
    n_x = n_mp // (n_core * 3)
    n_z = n_mp // (n_core * n_x)
    by_feature = exchange(enc_out, "segment", 1, n_seg, 0, True)
    features = by_feature.transpose(1, 2, 0, 3).reshape(nb, ns, n_seg * nd)
    by_z = exchange(features, "mp", n_x * n_core, n_z, 1, True)
    by_x = exchange(by_z, "mp", n_core, n_x, 2, True)
    by_core = exchange(by_x, "mp", 1, n_core, 3, True)
    encoder = by_core.transpose(3, 2, 1, 0, 4, 5).reshape(nb, n_mp * ns, n_seg * nd)
    keyval = jnp.einsum(
        "bsd,dch->bsch",
        encoder,
        keyval_w,
        preferred_element_type=jnp.float32,
    ).astype(jnp.bfloat16)
    total_src = keyval.shape[1]
    usable = jnp.arange(total_src)[None, :] < src_len[:, None]
    context, dkeyval = attend_pass(query, keyval, cotangent, usable)
    grad_blocks = dkeyval.reshape(nb, n_z, n_x, n_core, ns, *dkeyval.shape[2:])
    layer_grad = jnp.einsum(
        "bzxwsch,dch->wxzbsd", grad_blocks, keyval_w, preferred_element_type=jnp.float32
    )
    over_core = exchange(layer_grad, "mp", 1, n_core, 4, False).sum(axis=0)
    over_x = exchange(over_core, "mp", n_core, n_x, 5, False).sum(axis=0)
    by_heads = exchange(over_x, "mp", n_x * n_core, n_z, 6, False).sum(axis=0)
    split = by_heads.reshape(nb, ns, n_seg, nd).transpose(2, 0, 1, 3)
    d_enc = exchange(split, "segment", 1, n_seg, 7, False).sum(axis=0)
    return (context[:, None], d_enc)


def solution(mesh):
    placed = (
        P(None, "mp", "segment"),
        P(None, "segment", None, None),
        P(None, "segment", None, "mp"),
        P("segment", None, "mp"),
        P("segment", None, None, "mp"),
        P(),
    )
    return jax.shard_map(
        local,
        mesh=mesh,
        in_specs=placed,
        out_specs=(P(None, "segment", None, "mp"), P(None, "mp", "segment")),
        check_vma=False,
    )
```

```python
import math

import jax
import jax.numpy as jnp
from jax import lax
from jax.sharding import PartitionSpec as P
from jax.experimental import pallas as pl
from jax.experimental.pallas import tpu as pltpu
import functools

HD = 64


def attend_pass(query, keyval, cotangent, usable):
    num_batch, num_tgt, width = query.shape
    num_heads = width // HD
    inv_root = 1.0 / math.sqrt(HD)
    query_heads = query.reshape(num_batch, num_tgt, num_heads, HD)
    key_heads = keyval[:, :, 0].reshape(num_batch, -1, num_heads, HD)
    value_heads = keyval[:, :, 1].reshape(num_batch, -1, num_heads, HD)
    cot_heads = cotangent.reshape(num_batch, num_tgt, num_heads, HD)
    scores = (
        jnp.einsum("bthe,bshe->bhts", query_heads, key_heads, preferred_element_type=jnp.float32)
        * inv_root
    )
    scores = jnp.where(usable[:, None, None, :], scores, jnp.float32(-1e30))
    shifted = scores - jnp.max(scores, axis=-1, keepdims=True)
    raised = jnp.exp(shifted)
    attend = raised / jnp.sum(raised, axis=-1, keepdims=True)
    attend_low = attend.astype(jnp.bfloat16)
    context = jnp.einsum(
        "bhts,bshe->bthe", attend_low, value_heads, preferred_element_type=jnp.float32
    ).astype(jnp.bfloat16)
    slope = jnp.einsum(
        "bthe,bshe->bhts", cot_heads, value_heads, preferred_element_type=jnp.float32
    )
    row_dot = jnp.einsum("bthe,bthe->bht", cot_heads, context, preferred_element_type=jnp.float32)
    dscore = (attend * (slope - row_dot[..., None]) * inv_root).astype(jnp.bfloat16)
    dkey = jnp.einsum(
        "bhts,bthe->bshe", dscore, query_heads, preferred_element_type=jnp.float32
    ).astype(jnp.bfloat16)
    dvalue = jnp.einsum(
        "bhts,bthe->bshe", attend_low, cot_heads, preferred_element_type=jnp.float32
    ).astype(jnp.bfloat16)
    dkeyval = jnp.stack(
        [dkey.reshape(num_batch, -1, width), dvalue.reshape(num_batch, -1, width)], axis=2
    )
    return (context.reshape(num_batch, num_tgt, width), dkeyval)


def _exchange_kernel(axis, stride, count, gather, x_ref, y_ref, send_sem, recv_sem):
    me = lax.axis_index(axis)
    digit = lax.rem(lax.div(me, stride), count)
    base = me - digit * stride
    pieces = y_ref.shape[1]
    mesh_ids = pl.DeviceIdType.MESH
    barrier = pltpu.get_barrier_semaphore()

    def greet(k, carry):
        peer = base + lax.rem(digit + k, count) * stride
        pl.semaphore_signal(barrier, inc=1, device_id={axis: peer}, device_id_type=mesh_ids)
        return carry

    lax.fori_loop(1, count, greet, 0)
    pl.semaphore_wait(barrier, count - 1)

    def send(i, carry):
        k = 1 + lax.div(i, pieces)
        p = lax.rem(i, pieces)
        slot = lax.rem(digit + k, count)
        block = x_ref.at[p] if gather else x_ref.at[slot, p]
        pltpu.make_async_remote_copy(
            src_ref=block,
            dst_ref=y_ref.at[digit, p],
            send_sem=send_sem,
            recv_sem=recv_sem,
            device_id={axis: base + slot * stride},
            device_id_type=mesh_ids,
        ).start()
        return carry

    lax.fori_loop(0, (count - 1) * pieces, send, 0)
    every = pltpu.make_async_remote_copy(
        src_ref=y_ref.at[pl.ds(0, count - 1)],
        dst_ref=y_ref.at[pl.ds(0, count - 1)],
        send_sem=send_sem,
        recv_sem=recv_sem,
        device_id={axis: base + lax.rem(digit + 1, count) * stride},
        device_id_type=mesh_ids,
    )
    every.wait_send()
    every.wait_recv()


def exchange(x, axis, stride, count, cid, gather):
    block = x.shape if gather else x.shape[1:]
    lead = () if gather else (count,)
    pieces = math.prod(block[:-2])
    parts = x.reshape(lead + (pieces, -1) + tuple(block[-2:]))
    out_shape = jax.ShapeDtypeStruct((count,) + parts.shape[len(lead):], x.dtype)
    received = pl.pallas_call(
        functools.partial(_exchange_kernel, axis, stride, count, gather),
        out_shape=out_shape,
        in_specs=[pl.BlockSpec(memory_space=pl.ANY)],
        out_specs=pl.BlockSpec(memory_space=pl.ANY),
        scratch_shapes=[pltpu.SemaphoreType.DMA, pltpu.SemaphoreType.DMA],
        compiler_params=pltpu.CompilerParams(collective_id=cid, has_side_effects=True),
    )(parts).reshape((count,) + tuple(block))
    digit = lax.rem(lax.div(lax.axis_index(axis), stride), count)
    mine = (jnp.arange(count) == digit).reshape((count,) + (1,) * len(block))
    own = x[None] if gather else x
    return jnp.where(mine, own, received)


def local(enc_out, dec_in, grad_context, w_query, w_keyval, src_len):
    inputs = dec_in[:, 0]
    cotangent = grad_context[:, 0]
    query_w = w_query[0]
    keyval_w = w_keyval[0]
    query = jnp.einsum("btd,dh->bth", inputs, query_w, preferred_element_type=jnp.float32).astype(
        jnp.bfloat16
    )
    nb, ns, nd = enc_out.shape
    n_mp = lax.axis_size("mp")
    n_seg = lax.axis_size("segment")
    n_core = 2
    n_x = n_mp // (n_core * 3)
    n_z = n_mp // (n_core * n_x)
    by_feature = exchange(enc_out, "segment", 1, n_seg, 0, True)
    features = by_feature.transpose(1, 2, 0, 3).reshape(nb, ns, n_seg * nd)
    by_z = exchange(features, "mp", n_x * n_core, n_z, 1, True)
    by_x = exchange(by_z, "mp", n_core, n_x, 2, True)
    by_core = exchange(by_x, "mp", 1, n_core, 3, True)
    encoder = by_core.transpose(3, 2, 1, 0, 4, 5).reshape(nb, n_mp * ns, n_seg * nd)
    keyval = jnp.einsum(
        "bsd,dch->bsch",
        encoder,
        keyval_w,
        preferred_element_type=jnp.float32,
    ).astype(jnp.bfloat16)
    total_src = keyval.shape[1]
    usable = jnp.arange(total_src)[None, :] < src_len[:, None]
    context, dkeyval = attend_pass(query, keyval, cotangent, usable)
    grad_blocks = dkeyval.reshape(nb, n_z, n_x, n_core, ns, *dkeyval.shape[2:])
    layer_grad = jnp.einsum(
        "bzxwsch,dch->wxzbsd", grad_blocks, keyval_w, preferred_element_type=jnp.float32
    )
    over_core = exchange(layer_grad, "mp", 1, n_core, 4, False).sum(axis=0)
    over_x = exchange(over_core, "mp", n_core, n_x, 5, False).sum(axis=0)
    by_heads = exchange(over_x, "mp", n_x * n_core, n_z, 6, False).sum(axis=0)
    split = by_heads.reshape(nb, ns, n_seg, nd).transpose(2, 0, 1, 3)
    d_enc = exchange(split, "segment", 1, n_seg, 7, False).sum(axis=0)
    return (context[:, None], d_enc)


def solution(mesh):
    placed = (
        P(None, "mp", "segment"),
        P(None, "segment", None, None),
        P(None, "segment", None, "mp"),
        P("segment", None, "mp"),
        P("segment", None, None, "mp"),
        P(),
    )
    return jax.shard_map(
        local,
        mesh=mesh,
        in_specs=placed,
        out_specs=(P(None, "segment", None, "mp"), P(None, "mp", "segment")),
        check_vma=False,
    )
```

```python
import math

import jax
import jax.numpy as jnp
from jax import lax
from jax.sharding import PartitionSpec as P
from jax.experimental import pallas as pl
from jax.experimental.pallas import tpu as pltpu
import functools

HD = 64


def attend_pass(query, keyval, cotangent, usable):
    num_batch, num_tgt, width = query.shape
    num_heads = width // HD
    inv_root = 1.0 / math.sqrt(HD)
    query_heads = query.reshape(num_batch, num_tgt, num_heads, HD)
    key_heads = keyval[:, :, 0].reshape(num_batch, -1, num_heads, HD)
    value_heads = keyval[:, :, 1].reshape(num_batch, -1, num_heads, HD)
    cot_heads = cotangent.reshape(num_batch, num_tgt, num_heads, HD)
    scores = (
        jnp.einsum("bthe,bshe->bhts", query_heads, key_heads, preferred_element_type=jnp.float32)
        * inv_root
    )
    scores = jnp.where(usable[:, None, None, :], scores, jnp.float32(-1e30))
    shifted = scores - jnp.max(scores, axis=-1, keepdims=True)
    raised = jnp.exp(shifted)
    attend = raised / jnp.sum(raised, axis=-1, keepdims=True)
    attend_low = attend.astype(jnp.bfloat16)
    context = jnp.einsum(
        "bhts,bshe->bthe", attend_low, value_heads, preferred_element_type=jnp.float32
    ).astype(jnp.bfloat16)
    slope = jnp.einsum(
        "bthe,bshe->bhts", cot_heads, value_heads, preferred_element_type=jnp.float32
    )
    row_dot = jnp.einsum("bthe,bthe->bht", cot_heads, context, preferred_element_type=jnp.float32)
    dscore = (attend * (slope - row_dot[..., None]) * inv_root).astype(jnp.bfloat16)
    dkey = jnp.einsum(
        "bhts,bthe->bshe", dscore, query_heads, preferred_element_type=jnp.float32
    ).astype(jnp.bfloat16)
    dvalue = jnp.einsum(
        "bhts,bthe->bshe", attend_low, cot_heads, preferred_element_type=jnp.float32
    ).astype(jnp.bfloat16)
    dkeyval = jnp.stack(
        [dkey.reshape(num_batch, -1, width), dvalue.reshape(num_batch, -1, width)], axis=2
    )
    return (context.reshape(num_batch, num_tgt, width), dkeyval)


def _exchange_kernel(axis, stride, count, gather, x_ref, y_ref, send_sem, recv_sem):
    me = lax.axis_index(axis)
    digit = lax.rem(lax.div(me, stride), count)
    base = me - digit * stride
    pieces = y_ref.shape[1]
    mesh_ids = pl.DeviceIdType.MESH
    barrier = pltpu.get_barrier_semaphore()

    def greet(k, carry):
        peer = base + lax.rem(digit + k, count) * stride
        pl.semaphore_signal(barrier, inc=1, device_id={axis: peer}, device_id_type=mesh_ids)
        return carry

    lax.fori_loop(1, count, greet, 0)
    pl.semaphore_wait(barrier, count - 1)

    def send(i, carry):
        k = 1 + lax.div(i, pieces)
        p = lax.rem(i, pieces)
        slot = lax.rem(digit + k, count)
        block = x_ref.at[p] if gather else x_ref.at[slot, p]
        pltpu.make_async_remote_copy(
            src_ref=block,
            dst_ref=y_ref.at[digit, p],
            send_sem=send_sem,
            recv_sem=recv_sem,
            device_id={axis: base + slot * stride},
            device_id_type=mesh_ids,
        ).start()
        return carry

    lax.fori_loop(0, (count - 1) * pieces, send, 0)
    every = pltpu.make_async_remote_copy(
        src_ref=y_ref.at[pl.ds(0, count - 1)],
        dst_ref=y_ref.at[pl.ds(0, count - 1)],
        send_sem=send_sem,
        recv_sem=recv_sem,
        device_id={axis: base + lax.rem(digit + 1, count) * stride},
        device_id_type=mesh_ids,
    )
    every.wait_send()
    every.wait_recv()


def exchange(x, axis, stride, count, cid, gather, wire=None):
    block = x.shape if gather else x.shape[1:]
    lead = () if gather else (count,)
    pieces = math.prod(block[:-2])
    parts = x.astype(wire or x.dtype).reshape(lead + (pieces, -1) + tuple(block[-2:]))
    out_shape = jax.ShapeDtypeStruct((count,) + parts.shape[len(lead):], parts.dtype)
    received = pl.pallas_call(
        functools.partial(_exchange_kernel, axis, stride, count, gather),
        out_shape=out_shape,
        in_specs=[pl.BlockSpec(memory_space=pl.ANY)],
        out_specs=pl.BlockSpec(memory_space=pl.ANY),
        scratch_shapes=[pltpu.SemaphoreType.DMA, pltpu.SemaphoreType.DMA],
        compiler_params=pltpu.CompilerParams(collective_id=cid, has_side_effects=True),
    )(parts).reshape((count,) + tuple(block)).astype(x.dtype)
    digit = lax.rem(lax.div(lax.axis_index(axis), stride), count)
    mine = (jnp.arange(count) == digit).reshape((count,) + (1,) * len(block))
    own = x[None] if gather else x
    return jnp.where(mine, own, received)


def local(enc_out, dec_in, grad_context, w_query, w_keyval, src_len):
    inputs = dec_in[:, 0]
    cotangent = grad_context[:, 0]
    query_w = w_query[0]
    keyval_w = w_keyval[0]
    query = jnp.einsum("btd,dh->bth", inputs, query_w, preferred_element_type=jnp.float32).astype(
        jnp.bfloat16
    )
    nb, ns, nd = enc_out.shape
    n_mp = lax.axis_size("mp")
    n_seg = lax.axis_size("segment")
    n_core = 2
    n_x = n_mp // (n_core * 3)
    n_z = n_mp // (n_core * n_x)
    by_feature = exchange(enc_out, "segment", 1, n_seg, 0, True)
    features = by_feature.transpose(1, 2, 0, 3).reshape(nb, ns, n_seg * nd)
    by_z = exchange(features, "mp", n_x * n_core, n_z, 1, True)
    by_x = exchange(by_z, "mp", n_core, n_x, 2, True)
    by_core = exchange(by_x, "mp", 1, n_core, 3, True)
    encoder = by_core.transpose(3, 2, 1, 0, 4, 5).reshape(nb, n_mp * ns, n_seg * nd)
    keyval = jnp.einsum(
        "bsd,dch->bsch",
        encoder,
        keyval_w,
        preferred_element_type=jnp.float32,
    ).astype(jnp.bfloat16)
    total_src = keyval.shape[1]
    usable = jnp.arange(total_src)[None, :] < src_len[:, None]
    context, dkeyval = attend_pass(query, keyval, cotangent, usable)
    grad_blocks = dkeyval.reshape(nb, n_z, n_x, n_core, ns, *dkeyval.shape[2:])
    layer_grad = jnp.einsum(
        "bzxwsch,dch->wxzbsd", grad_blocks, keyval_w, preferred_element_type=jnp.float32
    )
    over_core = exchange(layer_grad, "mp", 1, n_core, 4, False, jnp.bfloat16).sum(axis=0)
    over_x = exchange(over_core, "mp", n_core, n_x, 5, False, jnp.bfloat16).sum(axis=0)
    by_heads = exchange(over_x, "mp", n_x * n_core, n_z, 6, False, jnp.bfloat16).sum(axis=0)
    split = by_heads.reshape(nb, ns, n_seg, nd).transpose(2, 0, 1, 3)
    d_enc = exchange(split, "segment", 1, n_seg, 7, False).sum(axis=0)
    return (context[:, None], d_enc)


def solution(mesh):
    placed = (
        P(None, "mp", "segment"),
        P(None, "segment", None, None),
        P(None, "segment", None, "mp"),
        P("segment", None, "mp"),
        P("segment", None, None, "mp"),
        P(),
    )
    return jax.shard_map(
        local,
        mesh=mesh,
        in_specs=placed,
        out_specs=(P(None, "segment", None, "mp"), P(None, "mp", "segment")),
        check_vma=False,
    )
```

```python
import math

import jax
import jax.numpy as jnp
from jax import lax
from jax.sharding import PartitionSpec as P
from jax.experimental import pallas as pl
from jax.experimental.pallas import tpu as pltpu
import functools

HD = 64


def attend_pass(query, keyval, cotangent, usable):
    num_batch, num_tgt, width = query.shape
    num_heads = width // HD
    inv_root = 1.0 / math.sqrt(HD)
    query_heads = query.reshape(num_batch, num_tgt, num_heads, HD)
    key_heads = keyval[:, :, 0].reshape(num_batch, -1, num_heads, HD)
    value_heads = keyval[:, :, 1].reshape(num_batch, -1, num_heads, HD)
    cot_heads = cotangent.reshape(num_batch, num_tgt, num_heads, HD)
    scores = (
        jnp.einsum("bthe,bshe->bhts", query_heads, key_heads, preferred_element_type=jnp.float32)
        * inv_root
    )
    scores = jnp.where(usable[:, None, None, :], scores, jnp.float32(-1e30))
    shifted = scores - jnp.max(scores, axis=-1, keepdims=True)
    raised = jnp.exp(shifted)
    attend = raised / jnp.sum(raised, axis=-1, keepdims=True)
    attend_low = attend.astype(jnp.bfloat16)
    context = jnp.einsum(
        "bhts,bshe->bthe", attend_low, value_heads, preferred_element_type=jnp.float32
    ).astype(jnp.bfloat16)
    slope = jnp.einsum(
        "bthe,bshe->bhts", cot_heads, value_heads, preferred_element_type=jnp.float32
    )
    row_dot = jnp.einsum("bthe,bthe->bht", cot_heads, context, preferred_element_type=jnp.float32)
    dscore = (attend * (slope - row_dot[..., None]) * inv_root).astype(jnp.bfloat16)
    dkey = jnp.einsum(
        "bhts,bthe->bshe", dscore, query_heads, preferred_element_type=jnp.float32
    ).astype(jnp.bfloat16)
    dvalue = jnp.einsum(
        "bhts,bthe->bshe", attend_low, cot_heads, preferred_element_type=jnp.float32
    ).astype(jnp.bfloat16)
    dkeyval = jnp.stack(
        [dkey.reshape(num_batch, -1, width), dvalue.reshape(num_batch, -1, width)], axis=2
    )
    return (context.reshape(num_batch, num_tgt, width), dkeyval)


def _exchange_kernel(axis, stride, count, gather, lanes, x_ref, y_ref, send_sem, recv_sem):
    me = lax.axis_index(axis)
    digit = lax.rem(lax.div(me, stride), count)
    base = me - digit * stride
    pieces = y_ref.shape[1]
    mesh_ids = pl.DeviceIdType.MESH
    barrier = pltpu.get_barrier_semaphore()

    def greet(k, carry):
        peer = base + lax.rem(digit + k, count) * stride
        pl.semaphore_signal(barrier, inc=1, device_id={axis: peer}, device_id_type=mesh_ids)
        return carry

    lax.fori_loop(1, count, greet, 0)
    pl.semaphore_wait(barrier, count - 1)

    width = y_ref.shape[-1] // lanes

    def send(i, carry):
        k = 1 + lax.div(i, pieces * lanes)
        p = lax.rem(lax.div(i, lanes), pieces)
        cols = pl.ds(pl.multiple_of(lax.rem(i, lanes) * width, width), width)
        slot = lax.rem(digit + k, count)
        block = x_ref.at[p, :, :, cols] if gather else x_ref.at[slot, p, :, :, cols]
        pltpu.make_async_remote_copy(
            src_ref=block,
            dst_ref=y_ref.at[digit, p, :, :, cols],
            send_sem=send_sem,
            recv_sem=recv_sem,
            device_id={axis: base + slot * stride},
            device_id_type=mesh_ids,
        ).start()
        return carry

    lax.fori_loop(0, (count - 1) * pieces * lanes, send, 0)
    every = pltpu.make_async_remote_copy(
        src_ref=y_ref.at[pl.ds(0, count - 1)],
        dst_ref=y_ref.at[pl.ds(0, count - 1)],
        send_sem=send_sem,
        recv_sem=recv_sem,
        device_id={axis: base + lax.rem(digit + 1, count) * stride},
        device_id_type=mesh_ids,
    )
    every.wait_send()
    every.wait_recv()


def exchange(x, axis, stride, count, cid, gather, wire=None, lanes=1):
    block = x.shape if gather else x.shape[1:]
    lead = () if gather else (count,)
    pieces = math.prod(block[:-2])
    parts = x.astype(wire or x.dtype).reshape(lead + (pieces, -1) + tuple(block[-2:]))
    out_shape = jax.ShapeDtypeStruct((count,) + parts.shape[len(lead):], parts.dtype)
    received = pl.pallas_call(
        functools.partial(_exchange_kernel, axis, stride, count, gather, lanes),
        out_shape=out_shape,
        in_specs=[pl.BlockSpec(memory_space=pl.ANY)],
        out_specs=pl.BlockSpec(memory_space=pl.ANY),
        scratch_shapes=[pltpu.SemaphoreType.DMA, pltpu.SemaphoreType.DMA],
        compiler_params=pltpu.CompilerParams(collective_id=cid, has_side_effects=True),
    )(parts).reshape((count,) + tuple(block)).astype(x.dtype)
    digit = lax.rem(lax.div(lax.axis_index(axis), stride), count)
    mine = (jnp.arange(count) == digit).reshape((count,) + (1,) * len(block))
    own = x[None] if gather else x
    return jnp.where(mine, own, received)


def local(enc_out, dec_in, grad_context, w_query, w_keyval, src_len):
    inputs = dec_in[:, 0]
    cotangent = grad_context[:, 0]
    query_w = w_query[0]
    keyval_w = w_keyval[0]
    query = jnp.einsum("btd,dh->bth", inputs, query_w, preferred_element_type=jnp.float32).astype(
        jnp.bfloat16
    )
    nb, ns, nd = enc_out.shape
    n_mp = lax.axis_size("mp")
    n_seg = lax.axis_size("segment")
    n_core = 2
    n_x = n_mp // (n_core * 3)
    n_z = n_mp // (n_core * n_x)
    by_feature = exchange(enc_out, "segment", 1, n_seg, 0, True)
    features = by_feature.transpose(1, 2, 0, 3).reshape(nb, ns, n_seg * nd)
    by_z = exchange(features, "mp", n_x * n_core, n_z, 1, True, lanes=8)
    by_x = exchange(by_z, "mp", n_core, n_x, 2, True, lanes=4)
    by_core = exchange(by_x, "mp", 1, n_core, 3, True)
    encoder = by_core.transpose(3, 2, 1, 0, 4, 5).reshape(nb, n_mp * ns, n_seg * nd)
    keyval = jnp.einsum(
        "bsd,dch->bsch",
        encoder,
        keyval_w,
        preferred_element_type=jnp.float32,
    ).astype(jnp.bfloat16)
    total_src = keyval.shape[1]
    usable = jnp.arange(total_src)[None, :] < src_len[:, None]
    context, dkeyval = attend_pass(query, keyval, cotangent, usable)
    grad_blocks = dkeyval.reshape(nb, n_z, n_x, n_core, ns, *dkeyval.shape[2:])
    layer_grad = jnp.einsum(
        "bzxwsch,dch->wxzbsd", grad_blocks, keyval_w, preferred_element_type=jnp.float32
    )
    over_core = exchange(layer_grad, "mp", 1, n_core, 4, False, jnp.bfloat16).sum(axis=0)
    over_x = exchange(over_core, "mp", n_core, n_x, 5, False, jnp.bfloat16, 4).sum(axis=0)
    by_heads = exchange(over_x, "mp", n_x * n_core, n_z, 6, False, jnp.bfloat16, 8).sum(axis=0)
    split = by_heads.reshape(nb, ns, n_seg, nd).transpose(2, 0, 1, 3)
    d_enc = exchange(split, "segment", 1, n_seg, 7, False).sum(axis=0)
    return (context[:, None], d_enc)


def solution(mesh):
    placed = (
        P(None, "mp", "segment"),
        P(None, "segment", None, None),
        P(None, "segment", None, "mp"),
        P("segment", None, "mp"),
        P("segment", None, None, "mp"),
        P(),
    )
    return jax.shard_map(
        local,
        mesh=mesh,
        in_specs=placed,
        out_specs=(P(None, "segment", None, "mp"), P(None, "mp", "segment")),
        check_vma=False,
    )
```

```python
import math

import jax
import jax.numpy as jnp
from jax import lax
from jax.sharding import PartitionSpec as P
from jax.experimental import pallas as pl
from jax.experimental.pallas import tpu as pltpu
import functools

HD = 64


def attend_pass(query, keyval, cotangent, usable):
    num_batch, num_tgt, width = query.shape
    num_heads = width // HD
    inv_root = 1.0 / math.sqrt(HD)
    query_heads = query.reshape(num_batch, num_tgt, num_heads, HD)
    key_heads = keyval[:, :, 0].reshape(num_batch, -1, num_heads, HD)
    value_heads = keyval[:, :, 1].reshape(num_batch, -1, num_heads, HD)
    cot_heads = cotangent.reshape(num_batch, num_tgt, num_heads, HD)
    scores = (
        jnp.einsum("bthe,bshe->bhts", query_heads, key_heads, preferred_element_type=jnp.float32)
        * inv_root
    )
    scores = jnp.where(usable[:, None, None, :], scores, jnp.float32(-1e30))
    shifted = scores - jnp.max(scores, axis=-1, keepdims=True)
    raised = jnp.exp(shifted)
    attend = raised / jnp.sum(raised, axis=-1, keepdims=True)
    attend_low = attend.astype(jnp.bfloat16)
    context = jnp.einsum(
        "bhts,bshe->bthe", attend_low, value_heads, preferred_element_type=jnp.float32
    ).astype(jnp.bfloat16)
    slope = jnp.einsum(
        "bthe,bshe->bhts", cot_heads, value_heads, preferred_element_type=jnp.float32
    )
    row_dot = jnp.einsum("bthe,bthe->bht", cot_heads, context, preferred_element_type=jnp.float32)
    dscore = (attend * (slope - row_dot[..., None]) * inv_root).astype(jnp.bfloat16)
    dkey = jnp.einsum(
        "bhts,bthe->bshe", dscore, query_heads, preferred_element_type=jnp.float32
    ).astype(jnp.bfloat16)
    dvalue = jnp.einsum(
        "bhts,bthe->bshe", attend_low, cot_heads, preferred_element_type=jnp.float32
    ).astype(jnp.bfloat16)
    dkeyval = jnp.stack(
        [dkey.reshape(num_batch, -1, width), dvalue.reshape(num_batch, -1, width)], axis=2
    )
    return (context.reshape(num_batch, num_tgt, width), dkeyval)


def _exchange_kernel(axis, stride, count, gather, x_ref, y_ref, send_sem, recv_sem):
    me = lax.axis_index(axis)
    digit = lax.rem(lax.div(me, stride), count)
    base = me - digit * stride
    pieces = y_ref.shape[1]
    mesh_ids = pl.DeviceIdType.MESH
    barrier = pltpu.get_barrier_semaphore()

    def greet(k, carry):
        peer = base + lax.rem(digit + k, count) * stride
        pl.semaphore_signal(barrier, inc=1, device_id={axis: peer}, device_id_type=mesh_ids)
        return carry

    lax.fori_loop(1, count, greet, 0)
    pl.semaphore_wait(barrier, count - 1)

    def send(i, carry):
        k = 1 + lax.div(i, pieces)
        p = lax.rem(i, pieces)
        slot = lax.rem(digit + k, count)
        block = x_ref.at[p] if gather else x_ref.at[slot, p]
        pltpu.make_async_remote_copy(
            src_ref=block,
            dst_ref=y_ref.at[digit, p],
            send_sem=send_sem,
            recv_sem=recv_sem,
            device_id={axis: base + slot * stride},
            device_id_type=mesh_ids,
        ).start()
        return carry

    lax.fori_loop(0, (count - 1) * pieces, send, 0)
    every = pltpu.make_async_remote_copy(
        src_ref=y_ref.at[pl.ds(0, count - 1)],
        dst_ref=y_ref.at[pl.ds(0, count - 1)],
        send_sem=send_sem,
        recv_sem=recv_sem,
        device_id={axis: base + lax.rem(digit + 1, count) * stride},
        device_id_type=mesh_ids,
    )
    every.wait_send()
    every.wait_recv()


def exchange(x, axis, stride, count, cid, gather, wire=None):
    block = x.shape if gather else x.shape[1:]
    lead = () if gather else (count,)
    pieces = math.prod(block[:-2])
    parts = x.astype(wire or x.dtype).reshape(lead + (pieces, -1) + tuple(block[-2:]))
    out_shape = jax.ShapeDtypeStruct((count,) + parts.shape[len(lead):], parts.dtype)
    received = pl.pallas_call(
        functools.partial(_exchange_kernel, axis, stride, count, gather),
        out_shape=out_shape,
        in_specs=[pl.BlockSpec(memory_space=pl.ANY)],
        out_specs=pl.BlockSpec(memory_space=pl.ANY),
        scratch_shapes=[pltpu.SemaphoreType.DMA, pltpu.SemaphoreType.DMA],
        compiler_params=pltpu.CompilerParams(collective_id=cid, has_side_effects=True),
    )(parts).reshape((count,) + tuple(block)).astype(x.dtype)
    digit = lax.rem(lax.div(lax.axis_index(axis), stride), count)
    mine = (jnp.arange(count) == digit).reshape((count,) + (1,) * len(block))
    own = x[None] if gather else x
    return jnp.where(mine, own, received)


def local(enc_out, dec_in, grad_context, w_query, w_keyval, src_len):
    inputs = dec_in[:, 0]
    cotangent = grad_context[:, 0]
    query_w = w_query[0]
    keyval_w = w_keyval[0]
    query = jnp.einsum("btd,dh->bth", inputs, query_w, preferred_element_type=jnp.float32).astype(
        jnp.bfloat16
    )
    nb, ns, nd = enc_out.shape
    n_mp = lax.axis_size("mp")
    n_seg = lax.axis_size("segment")
    n_core = 2
    n_x = n_mp // (n_core * 3)
    n_z = n_mp // (n_core * n_x)
    by_z = exchange(enc_out, "mp", n_x * n_core, n_z, 0, True)
    by_seg = exchange(by_z, "segment", 1, n_seg, 1, True)
    features = by_seg.transpose(1, 2, 3, 0, 4).reshape(n_z, nb, ns, n_seg * nd)
    by_x = exchange(features, "mp", n_core, n_x, 2, True)
    by_core = exchange(by_x, "mp", 1, n_core, 3, True)
    encoder = by_core.transpose(3, 2, 1, 0, 4, 5).reshape(nb, n_mp * ns, n_seg * nd)
    keyval = jnp.einsum(
        "bsd,dch->bsch",
        encoder,
        keyval_w,
        preferred_element_type=jnp.float32,
    ).astype(jnp.bfloat16)
    total_src = keyval.shape[1]
    usable = jnp.arange(total_src)[None, :] < src_len[:, None]
    context, dkeyval = attend_pass(query, keyval, cotangent, usable)
    grad_blocks = dkeyval.reshape(nb, n_z, n_x, n_core, ns, *dkeyval.shape[2:])
    layer_grad = jnp.einsum(
        "bzxwsch,dch->wxzbsd", grad_blocks, keyval_w, preferred_element_type=jnp.float32
    )
    over_core = exchange(layer_grad, "mp", 1, n_core, 4, False, jnp.bfloat16).sum(axis=0)
    over_x = exchange(over_core, "mp", n_core, n_x, 5, False, jnp.bfloat16).sum(axis=0)
    split = over_x.reshape(n_z, nb, ns, n_seg, nd).transpose(3, 0, 1, 2, 4)
    by_layer = exchange(split, "segment", 1, n_seg, 6, False, jnp.bfloat16).sum(axis=0)
    d_enc = exchange(by_layer, "mp", n_x * n_core, n_z, 7, False).sum(axis=0)
    return (context[:, None], d_enc)


def solution(mesh):
    placed = (
        P(None, "mp", "segment"),
        P(None, "segment", None, None),
        P(None, "segment", None, "mp"),
        P("segment", None, "mp"),
        P("segment", None, None, "mp"),
        P(),
    )
    return jax.shard_map(
        local,
        mesh=mesh,
        in_specs=placed,
        out_specs=(P(None, "segment", None, "mp"), P(None, "mp", "segment")),
        check_vma=False,
    )
```

```python
import math

import jax
import jax.numpy as jnp
from jax import lax
from jax.sharding import PartitionSpec as P
from jax.experimental import pallas as pl
from jax.experimental.pallas import tpu as pltpu
import functools

HD = 64


def attend_pass(query, keyval, cotangent, usable):
    num_batch, num_tgt, width = query.shape
    num_heads = width // HD
    inv_root = 1.0 / math.sqrt(HD)
    query_heads = query.reshape(num_batch, num_tgt, num_heads, HD)
    key_heads = keyval[:, :, 0].reshape(num_batch, -1, num_heads, HD)
    value_heads = keyval[:, :, 1].reshape(num_batch, -1, num_heads, HD)
    cot_heads = cotangent.reshape(num_batch, num_tgt, num_heads, HD)
    scores = (
        jnp.einsum("bthe,bshe->bhts", query_heads, key_heads, preferred_element_type=jnp.float32)
        * inv_root
    )
    scores = jnp.where(usable[:, None, None, :], scores, jnp.float32(-1e30))
    shifted = scores - jnp.max(scores, axis=-1, keepdims=True)
    raised = jnp.exp(shifted)
    attend = raised / jnp.sum(raised, axis=-1, keepdims=True)
    attend_low = attend.astype(jnp.bfloat16)
    context = jnp.einsum(
        "bhts,bshe->bthe", attend_low, value_heads, preferred_element_type=jnp.float32
    ).astype(jnp.bfloat16)
    slope = jnp.einsum(
        "bthe,bshe->bhts", cot_heads, value_heads, preferred_element_type=jnp.float32
    )
    row_dot = jnp.einsum("bthe,bthe->bht", cot_heads, context, preferred_element_type=jnp.float32)
    dscore = (attend * (slope - row_dot[..., None]) * inv_root).astype(jnp.bfloat16)
    dkey = jnp.einsum(
        "bhts,bthe->bshe", dscore, query_heads, preferred_element_type=jnp.float32
    ).astype(jnp.bfloat16)
    dvalue = jnp.einsum(
        "bhts,bthe->bshe", attend_low, cot_heads, preferred_element_type=jnp.float32
    ).astype(jnp.bfloat16)
    dkeyval = jnp.stack(
        [dkey.reshape(num_batch, -1, width), dvalue.reshape(num_batch, -1, width)], axis=2
    )
    return (context.reshape(num_batch, num_tgt, width), dkeyval)


def _exchange_kernel(axis, stride, count, inner, gather, x_ref, y_ref, send_sem, recv_sem):
    me = lax.axis_index(axis)
    digit = lax.rem(lax.div(me, stride), count)
    base = me - digit * stride
    n_inner = lax.axis_size(inner) if inner else 1
    mine = digit * n_inner + (lax.axis_index(inner) if inner else 0)
    total = count * n_inner
    pieces = y_ref.shape[1]
    mesh_ids = pl.DeviceIdType.MESH

    def device_of(slot):
        where = {axis: base + lax.div(slot, n_inner) * stride}
        if inner:
            where[inner] = lax.rem(slot, n_inner)
        return where

    barrier = pltpu.get_barrier_semaphore()

    def greet(k, carry):
        slot = lax.rem(mine + k, total)
        pl.semaphore_signal(barrier, inc=1, device_id=device_of(slot), device_id_type=mesh_ids)
        return carry

    lax.fori_loop(1, total, greet, 0)
    pl.semaphore_wait(barrier, total - 1)

    def send(i, carry):
        k = 1 + lax.div(i, pieces)
        p = lax.rem(i, pieces)
        slot = lax.rem(mine + k, total)
        block = x_ref.at[p] if gather else x_ref.at[slot, p]
        pltpu.make_async_remote_copy(
            src_ref=block,
            dst_ref=y_ref.at[mine, p],
            send_sem=send_sem,
            recv_sem=recv_sem,
            device_id=device_of(slot),
            device_id_type=mesh_ids,
        ).start()
        return carry

    lax.fori_loop(0, (total - 1) * pieces, send, 0)
    every = pltpu.make_async_remote_copy(
        src_ref=y_ref.at[pl.ds(0, total - 1)],
        dst_ref=y_ref.at[pl.ds(0, total - 1)],
        send_sem=send_sem,
        recv_sem=recv_sem,
        device_id=device_of(lax.rem(mine + 1, total)),
        device_id_type=mesh_ids,
    )
    every.wait_send()
    every.wait_recv()


def exchange(x, axis, stride, count, cid, gather, wire=None, inner=None):
    total = count * (lax.axis_size(inner) if inner else 1)
    block = x.shape if gather else x.shape[1:]
    lead = () if gather else (total,)
    pieces = math.prod(block[:-2])
    parts = x.astype(wire or x.dtype).reshape(lead + (pieces, -1) + tuple(block[-2:]))
    out_shape = jax.ShapeDtypeStruct((total,) + parts.shape[len(lead):], parts.dtype)
    received = pl.pallas_call(
        functools.partial(_exchange_kernel, axis, stride, count, inner, gather),
        out_shape=out_shape,
        in_specs=[pl.BlockSpec(memory_space=pl.ANY)],
        out_specs=pl.BlockSpec(memory_space=pl.ANY),
        scratch_shapes=[pltpu.SemaphoreType.DMA, pltpu.SemaphoreType.DMA],
        compiler_params=pltpu.CompilerParams(collective_id=cid, has_side_effects=True),
    )(parts).reshape((total,) + tuple(block)).astype(x.dtype)
    digit = lax.rem(lax.div(lax.axis_index(axis), stride), count)
    if inner:
        digit = digit * lax.axis_size(inner) + lax.axis_index(inner)
    mine = (jnp.arange(total) == digit).reshape((total,) + (1,) * len(block))
    own = x[None] if gather else x
    return jnp.where(mine, own, received)


def local(enc_out, dec_in, grad_context, w_query, w_keyval, src_len):
    inputs = dec_in[:, 0]
    cotangent = grad_context[:, 0]
    query_w = w_query[0]
    keyval_w = w_keyval[0]
    query = jnp.einsum("btd,dh->bth", inputs, query_w, preferred_element_type=jnp.float32).astype(
        jnp.bfloat16
    )
    nb, ns, nd = enc_out.shape
    n_mp = lax.axis_size("mp")
    n_seg = lax.axis_size("segment")
    n_core = 2
    n_x = n_mp // (n_core * 3)
    n_z = n_mp // (n_core * n_x)
    by_zs = exchange(enc_out, "mp", n_x * n_core, n_z, 0, True, inner="segment")
    features = (
        by_zs.reshape(n_z, n_seg, nb, ns, nd).transpose(0, 2, 3, 1, 4).reshape(n_z, nb, ns, n_seg * nd)
    )
    by_x = exchange(features, "mp", n_core, n_x, 2, True)
    by_core = exchange(by_x, "mp", 1, n_core, 3, True)
    encoder = by_core.transpose(3, 2, 1, 0, 4, 5).reshape(nb, n_mp * ns, n_seg * nd)
    keyval = jnp.einsum(
        "bsd,dch->bsch",
        encoder,
        keyval_w,
        preferred_element_type=jnp.float32,
    ).astype(jnp.bfloat16)
    total_src = keyval.shape[1]
    usable = jnp.arange(total_src)[None, :] < src_len[:, None]
    context, dkeyval = attend_pass(query, keyval, cotangent, usable)
    grad_blocks = dkeyval.reshape(nb, n_z, n_x, n_core, ns, *dkeyval.shape[2:])
    layer_grad = jnp.einsum(
        "bzxwsch,dch->wxzbsd", grad_blocks, keyval_w, preferred_element_type=jnp.float32
    )
    over_core = exchange(layer_grad, "mp", 1, n_core, 4, False, jnp.bfloat16).sum(axis=0)
    over_x = exchange(over_core, "mp", n_core, n_x, 5, False, jnp.bfloat16).sum(axis=0)
    split = (
        over_x.reshape(n_z, nb, ns, n_seg, nd).transpose(0, 3, 1, 2, 4).reshape(n_z * n_seg, nb, ns, nd)
    )
    d_enc = exchange(split, "mp", n_x * n_core, n_z, 6, False, jnp.bfloat16, inner="segment").sum(axis=0)
    return (context[:, None], d_enc)


def solution(mesh):
    placed = (
        P(None, "mp", "segment"),
        P(None, "segment", None, None),
        P(None, "segment", None, "mp"),
        P("segment", None, "mp"),
        P("segment", None, None, "mp"),
        P(),
    )
    return jax.shard_map(
        local,
        mesh=mesh,
        in_specs=placed,
        out_specs=(P(None, "segment", None, "mp"), P(None, "mp", "segment")),
        check_vma=False,
    )
```

```python
import math

import jax
import jax.numpy as jnp
from jax import lax
from jax.sharding import PartitionSpec as P
from jax.experimental import pallas as pl
from jax.experimental.pallas import tpu as pltpu
import functools

HD = 64


def attend_pass(query, keyval, cotangent, usable):
    num_batch, num_tgt, width = query.shape
    num_heads = width // HD
    inv_root = 1.0 / math.sqrt(HD)
    query_heads = query.reshape(num_batch, num_tgt, num_heads, HD)
    key_heads = keyval[:, :, 0].reshape(num_batch, -1, num_heads, HD)
    value_heads = keyval[:, :, 1].reshape(num_batch, -1, num_heads, HD)
    cot_heads = cotangent.reshape(num_batch, num_tgt, num_heads, HD)
    scores = (
        jnp.einsum("bthe,bshe->bhts", query_heads, key_heads, preferred_element_type=jnp.float32)
        * inv_root
    )
    scores = jnp.where(usable[:, None, None, :], scores, jnp.float32(-1e30))
    shifted = scores - jnp.max(scores, axis=-1, keepdims=True)
    raised = jnp.exp(shifted)
    attend = raised / jnp.sum(raised, axis=-1, keepdims=True)
    attend_low = attend.astype(jnp.bfloat16)
    context = jnp.einsum(
        "bhts,bshe->bthe", attend_low, value_heads, preferred_element_type=jnp.float32
    ).astype(jnp.bfloat16)
    slope = jnp.einsum(
        "bthe,bshe->bhts", cot_heads, value_heads, preferred_element_type=jnp.float32
    )
    row_dot = jnp.einsum("bthe,bthe->bht", cot_heads, context, preferred_element_type=jnp.float32)
    dscore = (attend * (slope - row_dot[..., None]) * inv_root).astype(jnp.bfloat16)
    dkey = jnp.einsum(
        "bhts,bthe->bshe", dscore, query_heads, preferred_element_type=jnp.float32
    ).astype(jnp.bfloat16)
    dvalue = jnp.einsum(
        "bhts,bthe->bshe", attend_low, cot_heads, preferred_element_type=jnp.float32
    ).astype(jnp.bfloat16)
    dkeyval = jnp.stack(
        [dkey.reshape(num_batch, -1, width), dvalue.reshape(num_batch, -1, width)], axis=2
    )
    return (context.reshape(num_batch, num_tgt, width), dkeyval)


def _exchange_kernel(axis, stride, count, inner, gather, x_ref, y_ref, send_sem, recv_sem):
    me = lax.axis_index(axis)
    digit = lax.rem(lax.div(me, stride), count)
    base = me - digit * stride
    n_inner = lax.axis_size(inner) if inner else 1
    mine = digit * n_inner + (lax.axis_index(inner) if inner else 0)
    total = count * n_inner
    pieces = y_ref.shape[1]
    mesh_ids = pl.DeviceIdType.MESH

    def device_of(slot):
        where = {axis: base + lax.div(slot, n_inner) * stride}
        if inner:
            where[inner] = lax.rem(slot, n_inner)
        return where

    barrier = pltpu.get_barrier_semaphore()

    def greet(k, carry):
        slot = lax.rem(mine + k, total)
        pl.semaphore_signal(barrier, inc=1, device_id=device_of(slot), device_id_type=mesh_ids)
        return carry

    lax.fori_loop(1, total, greet, 0)
    pl.semaphore_wait(barrier, total - 1)

    def send(i, carry):
        k = 1 + lax.div(i, pieces)
        p = lax.rem(i, pieces)
        slot = lax.rem(mine + k, total)
        block = x_ref.at[p] if gather else x_ref.at[slot, p]
        pltpu.make_async_remote_copy(
            src_ref=block,
            dst_ref=y_ref.at[mine, p],
            send_sem=send_sem,
            recv_sem=recv_sem,
            device_id=device_of(slot),
            device_id_type=mesh_ids,
        ).start()
        return carry

    lax.fori_loop(0, (total - 1) * pieces, send, 0)
    every = pltpu.make_async_remote_copy(
        src_ref=y_ref.at[pl.ds(0, total - 1)],
        dst_ref=y_ref.at[pl.ds(0, total - 1)],
        send_sem=send_sem,
        recv_sem=recv_sem,
        device_id=device_of(lax.rem(mine + 1, total)),
        device_id_type=mesh_ids,
    )
    every.wait_send()
    every.wait_recv()


def exchange(x, axis, stride, count, cid, gather, wire=None, inner=None):
    total = count * (lax.axis_size(inner) if inner else 1)
    block = x.shape if gather else x.shape[1:]
    lead = () if gather else (total,)
    pieces = math.prod(block[:-2])
    parts = x.astype(wire or x.dtype).reshape(lead + (pieces, -1) + tuple(block[-2:]))
    out_shape = jax.ShapeDtypeStruct((total,) + parts.shape[len(lead):], parts.dtype)
    received = pl.pallas_call(
        functools.partial(_exchange_kernel, axis, stride, count, inner, gather),
        out_shape=out_shape,
        in_specs=[pl.BlockSpec(memory_space=pl.ANY)],
        out_specs=pl.BlockSpec(memory_space=pl.ANY),
        scratch_shapes=[pltpu.SemaphoreType.DMA, pltpu.SemaphoreType.DMA],
        compiler_params=pltpu.CompilerParams(collective_id=cid, has_side_effects=True),
    )(parts).reshape((total,) + tuple(block)).astype(x.dtype)
    digit = lax.rem(lax.div(lax.axis_index(axis), stride), count)
    if inner:
        digit = digit * lax.axis_size(inner) + lax.axis_index(inner)
    mine = (jnp.arange(total) == digit).reshape((total,) + (1,) * len(block))
    own = x[None] if gather else x
    return jnp.where(mine, own, received)


def local(enc_out, dec_in, grad_context, w_query, w_keyval, src_len):
    inputs = dec_in[:, 0]
    cotangent = grad_context[:, 0]
    query_w = w_query[0]
    keyval_w = w_keyval[0]
    query = jnp.einsum("btd,dh->bth", inputs, query_w, preferred_element_type=jnp.float32).astype(
        jnp.bfloat16
    )
    nb, ns, nd = enc_out.shape
    n_mp = lax.axis_size("mp")
    n_seg = lax.axis_size("segment")
    n_core = 2
    n_x = n_mp // (n_core * 3)
    n_z = n_mp // (n_core * n_x)
    by_zs = exchange(enc_out, "mp", n_x * n_core, n_z, 0, True, inner="segment")
    features = (
        by_zs.reshape(n_z, n_seg, nb, ns, nd).transpose(0, 2, 3, 1, 4).reshape(n_z, nb, ns, n_seg * nd)
    )
    by_x = exchange(features, "mp", n_core, n_x, 2, True)
    by_core = exchange(by_x, "mp", 1, n_core, 3, True)
    keyval = (
        jnp.einsum("wxzbsd,dch->wxzbsch", by_core, keyval_w, preferred_element_type=jnp.float32)
        .astype(jnp.bfloat16)
        .transpose(3, 2, 1, 0, 4, 5, 6)
        .reshape(nb, n_mp * ns, *keyval_w.shape[1:])
    )
    total_src = keyval.shape[1]
    usable = jnp.arange(total_src)[None, :] < src_len[:, None]
    context, dkeyval = attend_pass(query, keyval, cotangent, usable)
    grad_blocks = dkeyval.reshape(nb, n_z, n_x, n_core, ns, *dkeyval.shape[2:]).transpose(3, 2, 1, 0, 4, 5, 6)
    layer_grad = jnp.einsum(
        "wxzbsch,dch->wxzbsd", grad_blocks, keyval_w, preferred_element_type=jnp.float32
    )
    over_core = exchange(layer_grad, "mp", 1, n_core, 4, False, jnp.bfloat16).sum(axis=0)
    over_x = exchange(over_core, "mp", n_core, n_x, 5, False, jnp.bfloat16).sum(axis=0)
    split = (
        over_x.reshape(n_z, nb, ns, n_seg, nd).transpose(0, 3, 1, 2, 4).reshape(n_z * n_seg, nb, ns, nd)
    )
    d_enc = exchange(split, "mp", n_x * n_core, n_z, 6, False, jnp.bfloat16, inner="segment").sum(axis=0)
    return (context[:, None], d_enc)


def solution(mesh):
    placed = (
        P(None, "mp", "segment"),
        P(None, "segment", None, None),
        P(None, "segment", None, "mp"),
        P("segment", None, "mp"),
        P("segment", None, None, "mp"),
        P(),
    )
    return jax.shard_map(
        local,
        mesh=mesh,
        in_specs=placed,
        out_specs=(P(None, "segment", None, "mp"), P(None, "mp", "segment")),
        check_vma=False,
    )
```

```python
import math

import jax
import jax.numpy as jnp
from jax import lax
from jax.sharding import PartitionSpec as P
from jax.experimental import pallas as pl
from jax.experimental.pallas import tpu as pltpu
import functools

HD = 64


def attend_pass(query, keyval, cotangent, usable):
    num_batch, num_tgt, width = query.shape
    num_heads = width // HD
    inv_root = 1.0 / math.sqrt(HD)
    query_heads = query.reshape(num_batch, num_tgt, num_heads, HD)
    key_heads = keyval[:, :, 0].reshape(num_batch, -1, num_heads, HD)
    value_heads = keyval[:, :, 1].reshape(num_batch, -1, num_heads, HD)
    cot_heads = cotangent.reshape(num_batch, num_tgt, num_heads, HD)
    scores = (
        jnp.einsum("bthe,bshe->bhts", query_heads, key_heads, preferred_element_type=jnp.float32)
        * inv_root
    )
    scores = jnp.where(usable[:, None, None, :], scores, jnp.float32(-1e30))
    shifted = scores - jnp.max(scores, axis=-1, keepdims=True)
    raised = jnp.exp(shifted)
    attend = raised / jnp.sum(raised, axis=-1, keepdims=True)
    attend_low = attend.astype(jnp.bfloat16)
    context = jnp.einsum(
        "bhts,bshe->bthe", attend_low, value_heads, preferred_element_type=jnp.float32
    ).astype(jnp.bfloat16)
    slope = jnp.einsum(
        "bthe,bshe->bhts", cot_heads, value_heads, preferred_element_type=jnp.float32
    )
    row_dot = jnp.einsum("bthe,bthe->bht", cot_heads, context, preferred_element_type=jnp.float32)
    dscore = (attend * (slope - row_dot[..., None]) * inv_root).astype(jnp.bfloat16)
    dkey = jnp.einsum(
        "bhts,bthe->bshe", dscore, query_heads, preferred_element_type=jnp.float32
    ).astype(jnp.bfloat16)
    dvalue = jnp.einsum(
        "bhts,bthe->bshe", attend_low, cot_heads, preferred_element_type=jnp.float32
    ).astype(jnp.bfloat16)
    dkeyval = jnp.stack(
        [dkey.reshape(num_batch, -1, width), dvalue.reshape(num_batch, -1, width)], axis=2
    )
    return (context.reshape(num_batch, num_tgt, width), dkeyval)


def _exchange_kernel(axis, stride, count, inner, gather, x_ref, y_ref, send_sem, recv_sem):
    me = lax.axis_index(axis)
    digit = lax.rem(lax.div(me, stride), count)
    base = me - digit * stride
    n_inner = lax.axis_size(inner) if inner else 1
    mine = digit * n_inner + (lax.axis_index(inner) if inner else 0)
    total = count * n_inner
    pieces = y_ref.shape[1]
    mesh_ids = pl.DeviceIdType.MESH

    def device_of(slot):
        where = {axis: base + lax.div(slot, n_inner) * stride}
        if inner:
            where[inner] = lax.rem(slot, n_inner)
        return where

    barrier = pltpu.get_barrier_semaphore()

    def greet(k, carry):
        slot = lax.rem(mine + k, total)
        pl.semaphore_signal(barrier, inc=1, device_id=device_of(slot), device_id_type=mesh_ids)
        return carry

    lax.fori_loop(1, total, greet, 0)
    pl.semaphore_wait(barrier, total - 1)

    def send(i, carry):
        k = 1 + lax.div(i, pieces)
        p = lax.rem(i, pieces)
        slot = lax.rem(mine + k, total)
        block = x_ref.at[p] if gather else x_ref.at[slot, p]
        pltpu.make_async_remote_copy(
            src_ref=block,
            dst_ref=y_ref.at[mine, p],
            send_sem=send_sem,
            recv_sem=recv_sem,
            device_id=device_of(slot),
            device_id_type=mesh_ids,
        ).start()
        return carry

    lax.fori_loop(0, (total - 1) * pieces, send, 0)
    every = pltpu.make_async_remote_copy(
        src_ref=y_ref.at[pl.ds(0, total - 1)],
        dst_ref=y_ref.at[pl.ds(0, total - 1)],
        send_sem=send_sem,
        recv_sem=recv_sem,
        device_id=device_of(lax.rem(mine + 1, total)),
        device_id_type=mesh_ids,
    )
    every.wait_send()
    every.wait_recv()


def exchange(x, axis, stride, count, cid, gather, wire=None, inner=None):
    total = count * (lax.axis_size(inner) if inner else 1)
    block = x.shape if gather else x.shape[1:]
    lead = () if gather else (total,)
    pieces = math.prod(block[:-2])
    parts = x.astype(wire or x.dtype).reshape(lead + (pieces, -1) + tuple(block[-2:]))
    out_shape = jax.ShapeDtypeStruct((total,) + parts.shape[len(lead):], parts.dtype)
    received = pl.pallas_call(
        functools.partial(_exchange_kernel, axis, stride, count, inner, gather),
        out_shape=out_shape,
        in_specs=[pl.BlockSpec(memory_space=pl.ANY)],
        out_specs=pl.BlockSpec(memory_space=pl.ANY),
        scratch_shapes=[pltpu.SemaphoreType.DMA, pltpu.SemaphoreType.DMA],
        compiler_params=pltpu.CompilerParams(collective_id=cid, has_side_effects=True),
    )(parts).reshape((total,) + tuple(block)).astype(x.dtype)
    digit = lax.rem(lax.div(lax.axis_index(axis), stride), count)
    if inner:
        digit = digit * lax.axis_size(inner) + lax.axis_index(inner)
    mine = (jnp.arange(total) == digit).reshape((total,) + (1,) * len(block))
    own = x[None] if gather else x
    return jnp.where(mine, own, received)


def local(enc_out, dec_in, grad_context, w_query, w_keyval, src_len):
    inputs = dec_in[:, 0]
    cotangent = grad_context[:, 0]
    query_w = w_query[0]
    keyval_w = w_keyval[0]
    query = jnp.einsum("btd,dh->bth", inputs, query_w, preferred_element_type=jnp.float32).astype(
        jnp.bfloat16
    )
    nb, ns, nd = enc_out.shape
    n_mp = lax.axis_size("mp")
    n_seg = lax.axis_size("segment")
    n_core = 2
    n_x = n_mp // (n_core * 3)
    n_z = n_mp // (n_core * n_x)
    by_zs = exchange(enc_out, "mp", n_x * n_core, n_z, 0, True, inner="segment")
    features = (
        by_zs.reshape(n_z, n_seg, nb, ns, nd).transpose(0, 2, 3, 1, 4).reshape(n_z, nb, ns, n_seg * nd)
    )
    by_x = exchange(features, "mp", n_core, n_x, 2, True)
    by_core = exchange(by_x, "mp", 1, n_core, 3, True)
    encoder = by_core.transpose(3, 2, 1, 0, 4, 5).reshape(nb, n_mp * ns, n_seg * nd)
    keyval = jnp.einsum(
        "bsd,dch->bsch",
        encoder,
        keyval_w,
        preferred_element_type=jnp.float32,
    ).astype(jnp.bfloat16)
    total_src = keyval.shape[1]
    usable = jnp.arange(total_src)[None, :] < src_len[:, None]
    context, dkeyval = attend_pass(query, keyval, cotangent, usable)
    grad_blocks = dkeyval.reshape(nb, n_z, n_x, n_core, ns, *dkeyval.shape[2:])
    layer_grad = jnp.einsum(
        "bzxwsch,dch->wxzbsd", grad_blocks, keyval_w, preferred_element_type=jnp.float32
    )
    over_core = exchange(layer_grad, "mp", 1, n_core, 4, False, jnp.bfloat16).sum(axis=0)
    over_x = exchange(over_core, "mp", n_core, n_x, 5, False, jnp.bfloat16).sum(axis=0)
    split = over_x.reshape(n_z, nb, ns, n_seg, nd).transpose(3, 0, 1, 2, 4)
    by_layer = exchange(split, "segment", 1, n_seg, 6, False, jnp.bfloat16).sum(axis=0)
    d_enc = exchange(by_layer, "mp", n_x * n_core, n_z, 7, False).sum(axis=0)
    return (context[:, None], d_enc)


def solution(mesh):
    placed = (
        P(None, "mp", "segment"),
        P(None, "segment", None, None),
        P(None, "segment", None, "mp"),
        P("segment", None, "mp"),
        P("segment", None, None, "mp"),
        P(),
    )
    return jax.shard_map(
        local,
        mesh=mesh,
        in_specs=placed,
        out_specs=(P(None, "segment", None, "mp"), P(None, "mp", "segment")),
        check_vma=False,
    )
```

```python
import math

import jax
import jax.numpy as jnp
from jax import lax
from jax.sharding import PartitionSpec as P
from jax.experimental import pallas as pl
from jax.experimental.pallas import tpu as pltpu
import functools

HD = 64


def attend_pass(query, keyval, cotangent, usable):
    num_batch, num_tgt, width = query.shape
    num_heads = width // HD
    inv_root = 1.0 / math.sqrt(HD)
    query_heads = query.reshape(num_batch, num_tgt, num_heads, HD)
    key_heads = keyval[:, :, 0].reshape(num_batch, -1, num_heads, HD)
    value_heads = keyval[:, :, 1].reshape(num_batch, -1, num_heads, HD)
    cot_heads = cotangent.reshape(num_batch, num_tgt, num_heads, HD)
    scores = (
        jnp.einsum("bthe,bshe->bhts", query_heads, key_heads, preferred_element_type=jnp.float32)
        * inv_root
    )
    scores = jnp.where(usable[:, None, None, :], scores, jnp.float32(-1e30))
    shifted = scores - jnp.max(scores, axis=-1, keepdims=True)
    raised = jnp.exp(shifted)
    attend = raised / jnp.sum(raised, axis=-1, keepdims=True)
    attend_low = attend.astype(jnp.bfloat16)
    context = jnp.einsum(
        "bhts,bshe->bthe", attend_low, value_heads, preferred_element_type=jnp.float32
    ).astype(jnp.bfloat16)
    slope = jnp.einsum(
        "bthe,bshe->bhts", cot_heads, value_heads, preferred_element_type=jnp.float32
    )
    row_dot = jnp.einsum("bthe,bthe->bht", cot_heads, context, preferred_element_type=jnp.float32)
    dscore = (attend * (slope - row_dot[..., None]) * inv_root).astype(jnp.bfloat16)
    dkey = jnp.einsum(
        "bhts,bthe->bshe", dscore, query_heads, preferred_element_type=jnp.float32
    ).astype(jnp.bfloat16)
    dvalue = jnp.einsum(
        "bhts,bthe->bshe", attend_low, cot_heads, preferred_element_type=jnp.float32
    ).astype(jnp.bfloat16)
    dkeyval = jnp.stack(
        [dkey.reshape(num_batch, -1, width), dvalue.reshape(num_batch, -1, width)], axis=2
    )
    return (context.reshape(num_batch, num_tgt, width), dkeyval)


def _exchange_kernel(axis, stride, count, inner, gather, x_ref, y_ref, send_sem, recv_sem):
    me = lax.axis_index(axis)
    digit = lax.rem(lax.div(me, stride), count)
    base = me - digit * stride
    n_inner = lax.axis_size(inner) if inner else 1
    mine = digit * n_inner + (lax.axis_index(inner) if inner else 0)
    total = count * n_inner
    pieces = y_ref.shape[1]
    mesh_ids = pl.DeviceIdType.MESH

    def device_of(slot):
        where = {axis: base + lax.div(slot, n_inner) * stride}
        if inner:
            where[inner] = lax.rem(slot, n_inner)
        return where

    barrier = pltpu.get_barrier_semaphore()

    def greet(k, carry):
        slot = lax.rem(mine + k, total)
        pl.semaphore_signal(barrier, inc=1, device_id=device_of(slot), device_id_type=mesh_ids)
        return carry

    lax.fori_loop(1, total, greet, 0)
    pl.semaphore_wait(barrier, total - 1)

    def send(i, carry):
        k = 1 + lax.rem(lax.div(i, pieces) + n_inner - 1, total - 1)
        p = lax.rem(i, pieces)
        slot = lax.rem(mine + k, total)
        block = x_ref.at[p] if gather else x_ref.at[slot, p]
        pltpu.make_async_remote_copy(
            src_ref=block,
            dst_ref=y_ref.at[mine, p],
            send_sem=send_sem,
            recv_sem=recv_sem,
            device_id=device_of(slot),
            device_id_type=mesh_ids,
        ).start()
        return carry

    lax.fori_loop(0, (total - 1) * pieces, send, 0)
    every = pltpu.make_async_remote_copy(
        src_ref=y_ref.at[pl.ds(0, total - 1)],
        dst_ref=y_ref.at[pl.ds(0, total - 1)],
        send_sem=send_sem,
        recv_sem=recv_sem,
        device_id=device_of(lax.rem(mine + 1, total)),
        device_id_type=mesh_ids,
    )
    every.wait_send()
    every.wait_recv()


def exchange(x, axis, stride, count, cid, gather, wire=None, inner=None):
    total = count * (lax.axis_size(inner) if inner else 1)
    block = x.shape if gather else x.shape[1:]
    lead = () if gather else (total,)
    pieces = math.prod(block[:-2])
    parts = x.astype(wire or x.dtype).reshape(lead + (pieces, -1) + tuple(block[-2:]))
    out_shape = jax.ShapeDtypeStruct((total,) + parts.shape[len(lead):], parts.dtype)
    received = pl.pallas_call(
        functools.partial(_exchange_kernel, axis, stride, count, inner, gather),
        out_shape=out_shape,
        in_specs=[pl.BlockSpec(memory_space=pl.ANY)],
        out_specs=pl.BlockSpec(memory_space=pl.ANY),
        scratch_shapes=[pltpu.SemaphoreType.DMA, pltpu.SemaphoreType.DMA],
        compiler_params=pltpu.CompilerParams(collective_id=cid, has_side_effects=True),
    )(parts).reshape((total,) + tuple(block)).astype(x.dtype)
    digit = lax.rem(lax.div(lax.axis_index(axis), stride), count)
    if inner:
        digit = digit * lax.axis_size(inner) + lax.axis_index(inner)
    mine = (jnp.arange(total) == digit).reshape((total,) + (1,) * len(block))
    own = x[None] if gather else x
    return jnp.where(mine, own, received)


def local(enc_out, dec_in, grad_context, w_query, w_keyval, src_len):
    inputs = dec_in[:, 0]
    cotangent = grad_context[:, 0]
    query_w = w_query[0]
    keyval_w = w_keyval[0]
    query = jnp.einsum("btd,dh->bth", inputs, query_w, preferred_element_type=jnp.float32).astype(
        jnp.bfloat16
    )
    nb, ns, nd = enc_out.shape
    n_mp = lax.axis_size("mp")
    n_seg = lax.axis_size("segment")
    n_core = 2
    n_x = n_mp // (n_core * 3)
    n_z = n_mp // (n_core * n_x)
    by_zs = exchange(enc_out, "mp", n_x * n_core, n_z, 0, True, inner="segment")
    features = (
        by_zs.reshape(n_z, n_seg, nb, ns, nd).transpose(0, 2, 3, 1, 4).reshape(n_z, nb, ns, n_seg * nd)
    )
    by_x = exchange(features, "mp", n_core, n_x, 2, True)
    by_core = exchange(by_x, "mp", 1, n_core, 3, True)
    encoder = by_core.transpose(3, 2, 1, 0, 4, 5).reshape(nb, n_mp * ns, n_seg * nd)
    keyval = jnp.einsum(
        "bsd,dch->bsch",
        encoder,
        keyval_w,
        preferred_element_type=jnp.float32,
    ).astype(jnp.bfloat16)
    total_src = keyval.shape[1]
    usable = jnp.arange(total_src)[None, :] < src_len[:, None]
    context, dkeyval = attend_pass(query, keyval, cotangent, usable)
    grad_blocks = dkeyval.reshape(nb, n_z, n_x, n_core, ns, *dkeyval.shape[2:])
    layer_grad = jnp.einsum(
        "bzxwsch,dch->wxzbsd", grad_blocks, keyval_w, preferred_element_type=jnp.float32
    )
    over_core = exchange(layer_grad, "mp", 1, n_core, 4, False, jnp.bfloat16).sum(axis=0)
    over_x = exchange(over_core, "mp", n_core, n_x, 5, False, jnp.bfloat16).sum(axis=0)
    split = (
        over_x.reshape(n_z, nb, ns, n_seg, nd).transpose(0, 3, 1, 2, 4).reshape(n_z * n_seg, nb, ns, nd)
    )
    d_enc = exchange(split, "mp", n_x * n_core, n_z, 6, False, jnp.bfloat16, inner="segment").sum(axis=0)
    return (context[:, None], d_enc)


def solution(mesh):
    placed = (
        P(None, "mp", "segment"),
        P(None, "segment", None, None),
        P(None, "segment", None, "mp"),
        P("segment", None, "mp"),
        P("segment", None, None, "mp"),
        P(),
    )
    return jax.shard_map(
        local,
        mesh=mesh,
        in_specs=placed,
        out_specs=(P(None, "segment", None, "mp"), P(None, "mp", "segment")),
        check_vma=False,
    )
```
